32 devices in a mesh: dp: 4 (over y, core), vocab: 8 (over z, x).
Axes of the slice: x: 2, y: 2, z: 4, core: 2. Of those that a mesh axis runs over, the one named last changes fastest.
Arguments:
- student_hidden: bfloat16 [2048, 2048], P('dp', 'vocab'), may hold values from -150 to 150
- teacher_hidden: bfloat16 [2048, 2048], P('dp', 'vocab'), may hold values from -150 to 150
- head: bfloat16 [2048, 16384], P(None, 'vocab'), may hold values from -0.375 to 0.375
- mask: int32 [2048], P('dp'), may hold values from 0 to 1
- steps: int32 [16], P('dp'), may hold values from 1 to 8
Outputs:
- divergence: float32 [2048], P('dp')
- hidden_grad: bfloat16 [2048, 2048], P('dp', 'vocab')
The draws below stay inside these ranges and needn't reach their ends.
All inputs are finite; a program needn't handle non-finite values.
Results may differ from the reference program's by a relative error of at most 0.0051.
Values may be sent and summed in bfloat16 or wider, within the bound.
A program may use at most 64 MiB of HBM per device.

```python
import jax
import jax.numpy as jnp
from jax import lax

D = 2048
LENGTH = 128
STEPS = 8
TOK_DEV = 512
SEQS = 16
TOKENS = 2048
VOCAB = 16384


def hidden_pair(key):
    shared = jnp.clip(jax.random.normal(jax.random.fold_in(key, 11), (TOKENS, D), jnp.float32), -4.0, 4.0)
    student_own = jnp.clip(jax.random.normal(jax.random.fold_in(key, 13), (TOKENS, D), jnp.float32), -4.0, 4.0)
    teacher_own = jnp.clip(jax.random.normal(jax.random.fold_in(key, 17), (TOKENS, D), jnp.float32), -4.0, 4.0)
    student = 0.8 * shared + 0.6 * student_own
    teacher = 0.8 * shared + 0.6 * teacher_own
    return (student, teacher)


def draw_student_hidden(key, part):
    return hidden_pair(key)[0].astype(jnp.bfloat16)


def draw_teacher_hidden(key, part):
    return hidden_pair(key)[1].astype(jnp.bfloat16)


def noise_pair(key):
    sequence = jnp.arange(SEQS, dtype=jnp.int32)
    jitter = jax.random.randint(jax.random.fold_in(key, 31), (SEQS,), 0, 2).astype(jnp.int32)
    noise_steps = jnp.minimum(1 + STEPS * sequence // SEQS + jitter, STEPS).astype(jnp.int32)
    levels = jax.random.randint(jax.random.fold_in(key, 37), (TOKENS,), 0, STEPS).astype(jnp.int32)
    masked = (levels < jnp.repeat(noise_steps, LENGTH)).astype(jnp.int32)
    return (masked, noise_steps)


def draw_mask(key, part):
    return noise_pair(key)[0]


def draw_steps(key, part):
    return noise_pair(key)[1]


def block_scale(own_key, extent, cuts, smallest, high):
    gain, own = 1.0, jax.random.fold_in(own_key, 6)
    for position, blocks in cuts:
        steps = jnp.exp(jax.random.uniform(jax.random.fold_in(own, position), (blocks,), jnp.float32, smallest / len(cuts), high / len(cuts)))
        gain = gain * jnp.repeat(steps, extent[position] // blocks).reshape([-1 if axis == position else 1 for axis in range(len(extent))])
    return gain


def scatter_about(rng, dims, deviation, reach, shards=(), kind=jnp.bfloat16):
    values = deviation * jax.random.normal(rng, dims, jnp.float32)
    if shards:
        values = values * block_scale(rng, dims, shards, -0.22, 0.18)
    return jnp.clip(values, -reach, reach).astype(kind)


def setup_inputs(seed: int = 0) -> dict:
    key_of = jax.random.split(jax.random.key(seed), 6)
    return {
        "student_hidden": draw_student_hidden(jax.random.fold_in(key_of[5], 71), 0),
        "teacher_hidden": draw_teacher_hidden(jax.random.fold_in(key_of[5], 71), 0),
        "head": scatter_about(key_of[2], (D, VOCAB), (D // 9) ** -0.5, 0.375, ((1, 8),)),
        "mask": draw_mask(jax.random.fold_in(key_of[5], 71), 0),
        "steps": draw_steps(jax.random.fold_in(key_of[5], 71), 0),
    }


def token_weights(mask, steps):
    masked = mask.astype(jnp.float32)
    factor = jnp.repeat(STEPS / steps.astype(jnp.float32), LENGTH)
    count = jnp.sum(masked)
    return masked * factor * (TOKENS / jnp.maximum(count, 1.0))


def reference(student_hidden, teacher_hidden, head, mask, steps):
    weight = token_weights(mask, steps)
    blocks = TOKENS // TOK_DEV

    def one_block(inputs):
        student_rows, teacher_rows, weight_rows = inputs
        student_log = jnp.dot(student_rows, head, preferred_element_type=jnp.float32)
        teacher_log = jnp.dot(teacher_rows, head, preferred_element_type=jnp.float32)
        student_peak = jnp.max(student_log, axis=1, keepdims=True)
        teacher_peak = jnp.max(teacher_log, axis=1, keepdims=True)
        student_exp = jnp.exp(student_log - student_peak)
        teacher_exp = jnp.exp(teacher_log - teacher_peak)
        student_total = jnp.sum(student_exp, axis=1, keepdims=True)
        teacher_total = jnp.sum(teacher_exp, axis=1, keepdims=True)
        cross = jnp.sum(teacher_exp * (teacher_log - student_log), axis=1, keepdims=True)
        kl_rows = cross / teacher_total - (teacher_peak + jnp.log(teacher_total)) + (student_peak + jnp.log(student_total))
        slopes = (weight_rows[:, None] * (student_exp / student_total - teacher_exp / teacher_total)).astype(jnp.bfloat16)
        grad_rows = jnp.dot(slopes, head.T, preferred_element_type=jnp.float32).astype(jnp.bfloat16)
        return kl_rows[:, 0], grad_rows

    kl_blocks, grad_blocks = lax.map(one_block, (student_hidden.reshape(blocks, TOK_DEV, D), teacher_hidden.reshape(blocks, TOK_DEV, D), weight.reshape(blocks, TOK_DEV)))
    return kl_blocks.reshape(TOKENS), grad_blocks.reshape(TOKENS, D)
```

```python
import functools

import jax
import jax.numpy as jnp
from jax import lax
from jax.experimental import pallas as pl
from jax.experimental.pallas import tpu as pltpu
from jax.sharding import PartitionSpec as P

MESH = pl.DeviceIdType.MESH
STEPS = 8
F32, BF16 = jnp.float32, jnp.bfloat16


def loop(start, stop, body):
    lax.fori_loop(start, stop, lambda i, carry: (body(i), carry)[1], 0)


def kernel(
    n, ndp, s_ref, t_ref, head_hbm, mask_ref, steps_ref, div_ref, grad_ref,
    head, s_all, t_all, s_log, t_log, slopes, cols, stats, counts, g, rs_out, rs_in,
    head_sem, ag_send, ag_recv, st_send, st_recv, ct_send, ct_recv, rs_send, rs_recv,
):
    T, F = s_ref.shape
    V = head.shape[1]
    H = n // 2
    C = T // 2
    me = lax.axis_index("vocab")
    dp = lax.axis_index("dp")

    def at_pos(q):
        q = lax.rem(q + 2 * n, n)
        x = q // H
        z = q + x * (n - 1 - 2 * q)
        return 2 * z + x

    z0, x0 = me // 2, lax.rem(me, 2)
    pos = z0 + x0 * (n - 1 - 2 * z0)
    ways = ((1, at_pos(pos + 1)), (-1, at_pos(pos - 1)))

    head_copy = pltpu.make_async_copy(head_hbm, head, head_sem)
    head_copy.start()

    count = jnp.sum(mask_ref[...].astype(F32), axis=1, keepdims=True)
    counts[dp] = jnp.broadcast_to(count, counts.shape[1:])

    barrier = pltpu.get_barrier_semaphore()
    for j in range(1, n):
        pl.semaphore_signal(barrier, 1, device_id={"vocab": lax.rem(me + j, n)}, device_id_type=MESH)
    for j in range(1, ndp):
        pl.semaphore_signal(barrier, 1, device_id={"dp": lax.rem(dp + j, ndp)}, device_id_type=MESH)
    pl.semaphore_wait(barrier, n - 1 + ndp - 1)

    def hop(way, h, which):
        step, target = ways[way]
        block = at_pos(pos - step * (h - 1))
        everything, own = ((s_all, s_ref), (t_all, t_ref))[which]
        source = own if isinstance(h, int) and h == 1 else everything.at[block]
        return pltpu.make_async_remote_copy(
            src_ref=source,
            dst_ref=everything.at[block],
            send_sem=ag_send.at[way, h, which],
            recv_sem=ag_recv.at[way, h, which],
            device_id={"vocab": target},
            device_id_type=MESH,
        )

    def arrived(way, h, which):
        hop(way, h, which).wait_recv()
        return at_pos(pos - ways[way][0] * h)

    for which in (0, 1):
        for way in (0, 1):
            hop(way, 1, which).start()

    def count_copy(j):
        return pltpu.make_async_remote_copy(
            src_ref=counts.at[dp],
            dst_ref=counts.at[dp],
            send_sem=ct_send.at[j],
            recv_sem=ct_recv.at[j],
            device_id={"dp": lax.rem(dp + j, ndp)},
            device_id_type=MESH,
        )

    for j in range(1, ndp):
        count_copy(j).start()

    W = 256

    def rows_of(block):
        return pl.ds(pl.multiple_of(block * F, F), F)

    def accumulate(log, parts, first=False):
        def tile(c):
            span = pl.ds(pl.multiple_of(c * W, W), W)
            total = None if first else log[:, span]
            for ref, block in parts:
                term = jnp.dot(ref[...], head[rows_of(block), span], preferred_element_type=F32)
                total = term if total is None else total + term
            log[:, span] = total

        loop(0, V // W, tile)

    head_copy.wait()
    accumulate(s_log, ((s_ref, me),), True)
    accumulate(t_log, ((t_ref, me),), True)

    def middle(h):
        for which, (everything, log) in enumerate(((s_all, s_log), (t_all, t_log))):
            found = []
            for way in (0, 1):
                block = arrived(way, h, which)
                if way == which:
                    hop(way, h + 1, which).start()
                else:
                    @pl.when(h + 1 < H)
                    def _():
                        hop(way, h + 1, which).start()
                found.append((everything.at[block], block))
            accumulate(log, found)

    loop(1, H, middle)
    block = arrived(0, H, 0)
    accumulate(s_log, ((s_all.at[block], block),))
    block = arrived(1, H, 1)
    accumulate(t_log, ((t_all.at[block], block),))

    R = 16
    lane = lax.broadcasted_iota(jnp.int32, (R, 128), 1)

    def softmax_rows(r):
        span = pl.ds(pl.multiple_of(r * R, R), R)
        s, t = s_log[span, :], t_log[span, :]
        s_peak = jnp.max(s, axis=1, keepdims=True)
        t_peak = jnp.max(t, axis=1, keepdims=True)
        s_exp = jnp.exp(s - s_peak)
        t_exp = jnp.exp(t - t_peak)
        cross = jnp.sum(t_exp * (t - s), axis=1, keepdims=True)
        s_log[span, :] = s_exp
        t_log[span, :] = t_exp
        s_sum = jnp.sum(s_exp, axis=1, keepdims=True)
        t_sum = jnp.sum(t_exp, axis=1, keepdims=True)
        value = jnp.where(lane == 0, s_peak, jnp.where(lane == 1, s_sum, jnp.where(
            lane == 2, t_peak, jnp.where(lane == 3, t_sum, cross))))
        cols[span, :] = value

    loop(0, T // R, softmax_rows)
    stats[me] = cols[...].T[:8, :]

    def stat_copy(j):
        return pltpu.make_async_remote_copy(
            src_ref=stats.at[me],
            dst_ref=stats.at[me],
            send_sem=st_send.at[j],
            recv_sem=st_recv.at[j],
            device_id={"vocab": lax.rem(me + j, n)},
            device_id_type=MESH,
        )

    for j in range(1, n):
        stat_copy(j).start()

    for j in range(1, ndp):
        count_copy(j).wait_recv()
    total = counts[0, :1, :1]
    for j in range(1, ndp):
        total = total + counts[j, :1, :1]
    segments = steps_ref.shape[0]
    factor = jnp.concatenate(
        [STEPS / jnp.full((1, T // segments), steps_ref[i], jnp.int32).astype(F32) for i in range(segments)], axis=1
    )
    weight = mask_ref[...].astype(F32) * factor * (T * ndp / jnp.maximum(total, 1.0))

    for j in range(1, n):
        stat_copy(j).wait_recv()
    s_top = stats[0, 0:1, :]
    t_top = stats[0, 2:3, :]
    for k in range(1, n):
        s_top = jnp.maximum(s_top, stats[k, 0:1, :])
        t_top = jnp.maximum(t_top, stats[k, 2:3, :])
    s_total = jnp.zeros((1, T), F32)
    t_total = jnp.zeros((1, T), F32)
    cross = jnp.zeros((1, T), F32)
    for k in range(n):
        t_scale = jnp.exp(stats[k, 2:3, :] - t_top)
        s_total += stats[k, 1:2, :] * jnp.exp(stats[k, 0:1, :] - s_top)
        t_total += stats[k, 3:4, :] * t_scale
        cross += stats[k, 4:5, :] * t_scale
    div_ref[...] = cross / t_total - (t_top + jnp.log(t_total)) + (s_top + jnp.log(s_total))
    mine = stats[me]
    s_factor = weight * (jnp.exp(mine[0:1, :] - s_top) / s_total)
    t_factor = weight * (jnp.exp(mine[2:3, :] - t_top) / t_total)
    row = lax.broadcasted_iota(jnp.int32, (128, T), 0)
    cols[...] = jnp.where(row == 0, s_factor, t_factor).T

    def slope_rows(r):
        span = pl.ds(pl.multiple_of(r * R, R), R)
        slopes[span, :] = (s_log[span, :] * cols[span, 0:1] - t_log[span, :] * cols[span, 1:2]).astype(BF16)

    loop(0, T // R, slope_rows)

    def part(block, c):
        return lax.dot_general(
            slopes[c * C:(c + 1) * C, :], head[rows_of(block), :], (((1,), (1,)), ((), ())), preferred_element_type=F32
        )

    def pass_on(way, k, c):
        return pltpu.make_async_remote_copy(
            src_ref=rs_out.at[way, k, c],
            dst_ref=rs_in.at[way, k, c],
            send_sem=rs_send.at[way, k, c],
            recv_sem=rs_recv.at[way, k, c],
            device_id={"vocab": ways[way][1]},
            device_id_type=MESH,
        )

    far = at_pos(pos + H)
    for c in (0, 1):
        rs_out[c, H, c] = part(far, c).astype(BF16)
        pass_on(c, H, c).start()

    def fill(k):
        for way in (0, 1):
            block = at_pos(pos + ways[way][0] * k)
            for c in (0, 1):
                g[way, c] = part(block, c)

    for way in (0, 1):
        block = at_pos(pos + ways[way][0] * (H - 1))
        c = 1 - way
        rs_out[way, H - 1, c] = part(block, c).astype(BF16)
        pass_on(way, H - 1, c).start()
        g[way, way] = part(block, way)
    for way in (0, 1):
        pass_on(way, H, way).wait_recv()
        rs_out[way, H - 1, way] = (g[way, way] + rs_in[way, H, way].astype(F32)).astype(BF16)
        pass_on(way, H - 1, way).start()

    def relay(i):
        k = H - 2 - i
        fill(k)
        for late in (0, 1):
            for way in (0, 1):
                c = 1 - way if late == 0 else way
                pass_on(way, k + 1, c).wait_recv()
                rs_out[way, k, c] = (g[way, c] + rs_in[way, k + 1, c].astype(F32)).astype(BF16)
                pass_on(way, k, c).start()

    loop(0, H - 2, relay)
    for c in (0, 1):
        g[0, c] = part(me, c)
    for c in (0, 1):
        for way in (0, 1):
            pass_on(way, 1, c).wait_recv()
        grad_ref[c * C:(c + 1) * C, :] = (
            g[0, c] + rs_in[0, 1, c].astype(F32) + rs_in[1, 1, c].astype(F32)
        ).astype(BF16)

    def left(h):
        for way in (0, 1):
            for which in (0, 1):
                hop(way, h, which).wait_send()

    for way in (0, 1):
        for which in (0, 1):
            hop(way, 1, which).wait_send()
    loop(2, H, left)
    for way in (0, 1):
        hop(way, H, way).wait_send()
    for j in range(1, ndp):
        count_copy(j).wait_send()
    for j in range(1, n):
        stat_copy(j).wait_send()
    for c in (0, 1):
        pass_on(c, H, c).wait_send()

    def gone(k):
        for way in (0, 1):
            for c in (0, 1):
                pass_on(way, k, c).wait_send()

    loop(1, H, gone)


def solution(mesh):
    n, ndp = mesh.shape["vocab"], mesh.shape["dp"]

    def per_device(student, teacher, head, mask, steps):
        T, F = student.shape
        D, V = head.shape
        H = n // 2
        vmem = pl.BlockSpec(memory_space=pltpu.VMEM)
        dma = pltpu.SemaphoreType.DMA
        div, grad = pl.pallas_call(
            functools.partial(kernel, n, ndp),
            out_shape=(jax.ShapeDtypeStruct((1, T), F32), jax.ShapeDtypeStruct((T, F), BF16)),
            in_specs=[vmem, vmem, pl.BlockSpec(memory_space=pl.ANY), vmem, pl.BlockSpec(memory_space=pltpu.SMEM)],
            out_specs=(vmem, vmem),
            scratch_shapes=[
                pltpu.VMEM((D, V), BF16),
                pltpu.VMEM((n, T, F), BF16),
                pltpu.VMEM((n, T, F), BF16),
                pltpu.VMEM((T, V), F32),
                pltpu.VMEM((T, V), F32),
                pltpu.VMEM((T, V), BF16),
                pltpu.VMEM((T, 128), F32),
                pltpu.VMEM((n, 8, T), F32),
                pltpu.VMEM((ndp, 8, 128), F32),
                pltpu.VMEM((2, 2, T // 2, F), F32),
                pltpu.VMEM((2, H + 1, 2, T // 2, F), BF16),
                pltpu.VMEM((2, H + 1, 2, T // 2, F), BF16),
                dma,
                dma((2, H + 1, 2)),
                dma((2, H + 1, 2)),
                dma((n,)),
                dma((n,)),
                dma((ndp,)),
                dma((ndp,)),
                dma((2, H + 1, 2)),
                dma((2, H + 1, 2)),
            ],
            compiler_params=pltpu.CompilerParams(
                collective_id=0, has_side_effects=True, vmem_limit_bytes=60 * 1024 * 1024
            ),
        )(student, teacher, head, mask.reshape(1, T), steps)
        return div.reshape(T), grad

    return jax.shard_map(
        per_device,
        mesh=mesh,
        in_specs=(P("dp", "vocab"), P("dp", "vocab"), P(None, "vocab"), P("dp"), P("dp")),
        out_specs=(P("dp"), P("dp", "vocab")),
        check_vma=False,
    )
```

```python
import functools

import jax
import jax.numpy as jnp
from jax import lax
from jax.experimental import pallas as pl
from jax.experimental.pallas import tpu as pltpu
from jax.sharding import PartitionSpec as P

MESH = pl.DeviceIdType.MESH
STEPS = 8
F32, BF16 = jnp.float32, jnp.bfloat16


def loop(start, stop, body):
    lax.fori_loop(start, stop, lambda i, carry: (body(i), carry)[1], 0)


def kernel(
    n, ndp, s_ref, t_ref, head_hbm, mask_ref, steps_ref, div_ref, grad_ref,
    head, s_all, t_all, s_log, t_log, slopes, cols, stats, counts, g, rs_out, rs_in,
    head_sem, ag_send, ag_recv, st_send, st_recv, ct_send, ct_recv, rs_send, rs_recv,
):
    T, F = s_ref.shape
    V = head.shape[1]
    H = n // 2
    C = T // 2
    E = C // 2
    me = lax.axis_index("vocab")
    dp = lax.axis_index("dp")

    def at_pos(q):
        q = lax.rem(q + 2 * n, n)
        x = q // H
        z = q + x * (n - 1 - 2 * q)
        return 2 * z + x

    z0, x0 = me // 2, lax.rem(me, 2)
    pos = z0 + x0 * (n - 1 - 2 * z0)
    ways = ((1, at_pos(pos + 1)), (-1, at_pos(pos - 1)))

    head_copy = pltpu.make_async_copy(head_hbm, head, head_sem)
    head_copy.start()

    count = jnp.sum(mask_ref[...].astype(F32), axis=1, keepdims=True)
    counts[dp] = jnp.broadcast_to(count, counts.shape[1:])

    barrier = pltpu.get_barrier_semaphore()
    for j in range(1, n):
        pl.semaphore_signal(barrier, 1, device_id={"vocab": lax.rem(me + j, n)}, device_id_type=MESH)
    for j in range(1, ndp):
        pl.semaphore_signal(barrier, 1, device_id={"dp": lax.rem(dp + j, ndp)}, device_id_type=MESH)
    pl.semaphore_wait(barrier, n - 1 + ndp - 1)

    def hop(a, way, h, which):
        step, target = ways[way]
        block = at_pos(pos - step * (h - 1))
        everything, own = ((s_all, s_ref), (t_all, t_ref))[which]
        source = own.at[a * C:(a + 1) * C] if isinstance(h, int) and h == 1 else everything.at[a, block]
        return pltpu.make_async_remote_copy(
            src_ref=source,
            dst_ref=everything.at[a, block],
            send_sem=ag_send.at[a, way, h, which],
            recv_sem=ag_recv.at[a, way, h, which],
            device_id={"vocab": target},
            device_id_type=MESH,
        )

    def arrived(a, way, h, which):
        hop(a, way, h, which).wait_recv()
        return at_pos(pos - ways[way][0] * h)

    def begin(a):
        for which in (0, 1):
            for way in (0, 1):
                hop(a, way, 1, which).start()

    begin(0)

    def count_copy(j):
        return pltpu.make_async_remote_copy(
            src_ref=counts.at[dp],
            dst_ref=counts.at[dp],
            send_sem=ct_send.at[j],
            recv_sem=ct_recv.at[j],
            device_id={"dp": lax.rem(dp + j, ndp)},
            device_id_type=MESH,
        )

    for j in range(1, ndp):
        count_copy(j).start()

    W = 256
    logs = (s_log, t_log)
    alls = (s_all, t_all)

    def rows_of(block):
        return pl.ds(pl.multiple_of(block * F, F), F)

    def accumulate(a, log, blocks, everything):
        half = slice(a * C, (a + 1) * C)

        def tile(c):
            span = pl.ds(pl.multiple_of(c * W, W), W)
            total = log[half, span]
            for block in blocks:
                total = total + jnp.dot(
                    everything[a, block], head[rows_of(block), span], preferred_element_type=F32
                )
            log[half, span] = total

        loop(0, V // W, tile)

    def first(log, own):
        def tile(c):
            span = pl.ds(pl.multiple_of(c * W, W), W)
            log[:, span] = jnp.dot(own[...], head[rows_of(me), span], preferred_element_type=F32)

        loop(0, V // W, tile)

    def take(a, h, which):
        found = []
        for way in (0, 1):
            if isinstance(h, int) and h == H and way != which:
                continue
            found.append(arrived(a, way, h, which))
            if isinstance(h, int):
                if h < H and (way == which or h + 1 < H):
                    hop(a, way, h + 1, which).start()
            else:
                hop(a, way, h + 1, which).start()
        accumulate(a, logs[which], found, alls[which])

    R = 16
    lane = lax.broadcasted_iota(jnp.int32, (R, 128), 1)

    def softmax_rows(r):
        span = pl.ds(pl.multiple_of(r * R, R), R)
        s, t = s_log[span, :], t_log[span, :]
        s_peak = jnp.max(s, axis=1, keepdims=True)
        t_peak = jnp.max(t, axis=1, keepdims=True)
        s_exp = jnp.exp(s - s_peak)
        t_exp = jnp.exp(t - t_peak)
        cross = jnp.sum(t_exp * (t - s), axis=1, keepdims=True)
        s_log[span, :] = s_exp
        t_log[span, :] = t_exp
        s_sum = jnp.sum(s_exp, axis=1, keepdims=True)
        t_sum = jnp.sum(t_exp, axis=1, keepdims=True)
        value = jnp.where(lane == 0, s_peak, jnp.where(lane == 1, s_sum, jnp.where(
            lane == 2, t_peak, jnp.where(lane == 3, t_sum, cross))))
        cols[span, :] = value

    def softmax(a, part):
        loop((a * C + part * E) // R, (a * C + part * E + E) // R, softmax_rows)

    def stat_copy(a, j):
        return pltpu.make_async_remote_copy(
            src_ref=stats.at[a, me],
            dst_ref=stats.at[a, me],
            send_sem=st_send.at[a, j],
            recv_sem=st_recv.at[a, j],
            device_id={"vocab": lax.rem(me + j, n)},
            device_id_type=MESH,
        )

    def tell(a):
        stats[a, me] = cols[a * C:(a + 1) * C, :].T[:8, :]
        for j in range(1, n):
            stat_copy(a, j).start()

    def slope_rows(r):
        span = pl.ds(pl.multiple_of(r * R, R), R)
        slopes[span, :] = (s_log[span, :] * cols[span, 0:1] - t_log[span, :] * cols[span, 1:2]).astype(BF16)

    def merge(a):
        half = slice(a * C, (a + 1) * C)
        if a == 0:
            for j in range(1, ndp):
                count_copy(j).wait_recv()
        total = counts[0, :1, :1]
        for j in range(1, ndp):
            total = total + counts[j, :1, :1]
        segments = steps_ref.shape[0] // 2
        factor = jnp.concatenate(
            [
                STEPS / jnp.full((1, C // segments), steps_ref[a * segments + i], jnp.int32).astype(F32)
                for i in range(segments)
            ],
            axis=1,
        )
        weight = mask_ref[:, half].astype(F32) * factor * (T * ndp / jnp.maximum(total, 1.0))
        for j in range(1, n):
            stat_copy(a, j).wait_recv()
        s_top = stats[a, 0, 0:1, :]
        t_top = stats[a, 0, 2:3, :]
        for k in range(1, n):
            s_top = jnp.maximum(s_top, stats[a, k, 0:1, :])
            t_top = jnp.maximum(t_top, stats[a, k, 2:3, :])
        s_total = jnp.zeros((1, C), F32)
        t_total = jnp.zeros((1, C), F32)
        cross = jnp.zeros((1, C), F32)
        for k in range(n):
            t_scale = jnp.exp(stats[a, k, 2:3, :] - t_top)
            s_total += stats[a, k, 1:2, :] * jnp.exp(stats[a, k, 0:1, :] - s_top)
            t_total += stats[a, k, 3:4, :] * t_scale
            cross += stats[a, k, 4:5, :] * t_scale
        div_ref[:, half] = cross / t_total - (t_top + jnp.log(t_total)) + (s_top + jnp.log(s_total))
        mine = stats[a, me]
        s_factor = weight * (jnp.exp(mine[0:1, :] - s_top) / s_total)
        t_factor = weight * (jnp.exp(mine[2:3, :] - t_top) / t_total)
        row = lax.broadcasted_iota(jnp.int32, (128, C), 0)
        cols[half, :] = jnp.where(row == 0, s_factor, t_factor).T
        loop(a * C // R, (a + 1) * C // R, slope_rows)

    def part(a, block):
        return lax.dot_general(
            slopes[a * C:(a + 1) * C, :], head[rows_of(block), :], (((1,), (1,)), ((), ())),
            preferred_element_type=F32,
        )

    def pass_on(a, way, k, c):
        return pltpu.make_async_remote_copy(
            src_ref=rs_out.at[a, way, k, c],
            dst_ref=rs_in.at[a, way, k, c],
            send_sem=rs_send.at[a, way, k, c],
            recv_sem=rs_recv.at[a, way, k, c],
            device_id={"vocab": ways[way][1]},
            device_id_type=MESH,
        )

    def far(a):
        whole = part(a, at_pos(pos + H)).astype(BF16)
        for c in (0, 1):
            rs_out[a, c, H, c] = whole[c * E:(c + 1) * E]
            pass_on(a, c, H, c).start()

    def fill(a, k):
        for way in (0, 1):
            whole = part(a, at_pos(pos + ways[way][0] * k))
            g[way, k, 0] = whole[:E]
            g[way, k, 1] = whole[E:]

    def own(a):
        whole = part(a, me)
        g[0, 0, 0] = whole[:E]
        g[0, 0, 1] = whole[E:]

    def relay_top(a):
        k = H - 1
        for way in (0, 1):
            c = 1 - way
            rs_out[a, way, k, c] = g[way, k, c].astype(BF16)
            pass_on(a, way, k, c).start()
        for way in (0, 1):
            pass_on(a, way, H, way).wait_recv()
            rs_out[a, way, k, way] = (g[way, k, way] + rs_in[a, way, H, way].astype(F32)).astype(BF16)
            pass_on(a, way, k, way).start()

    def relay(a, k):
        for late in (0, 1):
            for way in (0, 1):
                c = 1 - way if late == 0 else way
                pass_on(a, way, k + 1, c).wait_recv()
                rs_out[a, way, k, c] = (g[way, k, c] + rs_in[a, way, k + 1, c].astype(F32)).astype(BF16)
                pass_on(a, way, k, c).start()

    def finish(a):
        for c in (0, 1):
            for way in (0, 1):
                pass_on(a, way, 1, c).wait_recv()
            grad_ref[a * C + c * E:a * C + (c + 1) * E, :] = (
                g[0, 0, c] + rs_in[a, 0, 1, c].astype(F32) + rs_in[a, 1, 1, c].astype(F32)
            ).astype(BF16)

    head_copy.wait()
    first(s_log, s_ref)
    first(t_log, t_ref)

    loop(1, H - 1, lambda h: [take(0, h, which) for which in (0, 1)])
    for which in (0, 1):
        take(0, H - 1, which)
    begin(1)
    for which in (0, 1):
        take(0, H, which)

    take(1, 1, 0)
    softmax(0, 0)
    take(1, 1, 1)
    softmax(0, 1)
    tell(0)
    loop(2, H - 1, lambda h: [take(1, h, which) for which in (0, 1)])
    take(1, H - 1, 0)
    merge(0)
    take(1, H - 1, 1)
    far(0)
    fill(0, H - 1)
    take(1, H, 0)
    loop(1, H - 1, lambda k: fill(0, k))
    take(1, H, 1)
    relay_top(0)

    lower = list(range(H - 2, 0, -1))
    cut = len(lower) // 2
    softmax(1, 0)
    for k in lower[:cut]:
        relay(0, k)
    softmax(1, 1)
    tell(1)
    for k in lower[cut:]:
        relay(0, k)
    own(0)
    merge(1)
    far(1)
    finish(0)
    fill(1, H - 1)
    relay_top(1)

    def rest(i):
        fill(1, H - 2 - i)
        relay(1, H - 2 - i)

    loop(0, H - 2, rest)
    own(1)
    finish(1)

    for a in (0, 1):
        def left(h):
            for way in (0, 1):
                for which in (0, 1):
                    hop(a, way, h, which).wait_send()

        def gone(k):
            for way in (0, 1):
                for c in (0, 1):
                    pass_on(a, way, k, c).wait_send()

        left(1)
        loop(2, H, left)
        loop(1, H, gone)
        for way in (0, 1):
            hop(a, way, H, way).wait_send()
            pass_on(a, way, H, way).wait_send()
        for j in range(1, n):
            stat_copy(a, j).wait_send()
    for j in range(1, ndp):
        count_copy(j).wait_send()


def solution(mesh):
    n, ndp = mesh.shape["vocab"], mesh.shape["dp"]

    def per_device(student, teacher, head, mask, steps):
        T, F = student.shape
        D, V = head.shape
        H = n // 2
        vmem = pl.BlockSpec(memory_space=pltpu.VMEM)
        dma = pltpu.SemaphoreType.DMA
        div, grad = pl.pallas_call(
            functools.partial(kernel, n, ndp),
            out_shape=(jax.ShapeDtypeStruct((1, T), F32), jax.ShapeDtypeStruct((T, F), BF16)),
            in_specs=[vmem, vmem, pl.BlockSpec(memory_space=pl.ANY), vmem, pl.BlockSpec(memory_space=pltpu.SMEM)],
            out_specs=(vmem, vmem),
            scratch_shapes=[
                pltpu.VMEM((D, V), BF16),
                pltpu.VMEM((2, n, T // 2, F), BF16),
                pltpu.VMEM((2, n, T // 2, F), BF16),
                pltpu.VMEM((T, V), F32),
                pltpu.VMEM((T, V), F32),
                pltpu.VMEM((T, V), BF16),
                pltpu.VMEM((T, 128), F32),
                pltpu.VMEM((2, n, 8, T // 2), F32),
                pltpu.VMEM((ndp, 8, 128), F32),
                pltpu.VMEM((2, H, 2, T // 4, F), F32),
                pltpu.VMEM((2, 2, H + 1, 2, T // 4, F), BF16),
                pltpu.VMEM((2, 2, H + 1, 2, T // 4, F), BF16),
                dma,
                dma((2, 2, H + 1, 2)),
                dma((2, 2, H + 1, 2)),
                dma((2, n)),
                dma((2, n)),
                dma((ndp,)),
                dma((ndp,)),
                dma((2, 2, H + 1, 2)),
                dma((2, 2, H + 1, 2)),
            ],
            compiler_params=pltpu.CompilerParams(
                collective_id=0, has_side_effects=True, vmem_limit_bytes=60 * 1024 * 1024
            ),
        )(student, teacher, head, mask.reshape(1, T), steps)
        return div.reshape(T), grad

    return jax.shard_map(
        per_device,
        mesh=mesh,
        in_specs=(P("dp", "vocab"), P("dp", "vocab"), P(None, "vocab"), P("dp"), P("dp")),
        out_specs=(P("dp"), P("dp", "vocab")),
        check_vma=False,
    )
```

```python
import functools

import jax
import jax.numpy as jnp
from jax import lax
from jax.experimental import pallas as pl
from jax.experimental.pallas import tpu as pltpu
from jax.sharding import PartitionSpec as P

MESH = pl.DeviceIdType.MESH
STEPS = 8
F32, BF16 = jnp.float32, jnp.bfloat16


def loop(start, stop, body, unroll=1):
    lax.fori_loop(start, stop, lambda i, carry: (body(i), carry)[1], 0, unroll=unroll)


def kernel(
    n, ndp, s_ref, t_ref, head_hbm, mask_ref, steps_ref, div_ref, grad_ref,
    head, s_all, t_all, s_log, t_log, slopes, cols, stats, counts, g, rs_out, rs_in,
    head_sem, ag_send, ag_recv, st_send, st_recv, ct_send, ct_recv, rs_send, rs_recv,
):
    T, F = s_ref.shape
    V = head.shape[1]
    H = n // 2
    C = T // 2
    E = C // 2
    me = lax.axis_index("vocab")
    dp = lax.axis_index("dp")

    def at_pos(q):
        q = lax.rem(q + 2 * n, n)
        x = q // H
        z = q + x * (n - 1 - 2 * q)
        return 2 * z + x

    z0, x0 = me // 2, lax.rem(me, 2)
    pos = z0 + x0 * (n - 1 - 2 * z0)
    ways = ((1, at_pos(pos + 1)), (-1, at_pos(pos - 1)))

    head_copy = pltpu.make_async_copy(head_hbm, head, head_sem)
    head_copy.start()

    count = jnp.sum(mask_ref[...].astype(F32), axis=1, keepdims=True)
    counts[dp] = jnp.broadcast_to(count, counts.shape[1:])

    barrier = pltpu.get_barrier_semaphore()
    for j in range(1, n):
        pl.semaphore_signal(barrier, 1, device_id={"vocab": lax.rem(me + j, n)}, device_id_type=MESH)
    for j in range(1, ndp):
        pl.semaphore_signal(barrier, 1, device_id={"dp": lax.rem(dp + j, ndp)}, device_id_type=MESH)
    pl.semaphore_wait(barrier, n - 1 + ndp - 1)

    def hop(a, way, h, which):
        step, target = ways[way]
        block = at_pos(pos - step * (h - 1))
        everything, own = ((s_all, s_ref), (t_all, t_ref))[which]
        source = own.at[a * C:(a + 1) * C] if isinstance(h, int) and h == 1 else everything.at[a, block]
        return pltpu.make_async_remote_copy(
            src_ref=source,
            dst_ref=everything.at[a, block],
            send_sem=ag_send.at[a, way, h, which],
            recv_sem=ag_recv.at[a, way, h, which],
            device_id={"vocab": target},
            device_id_type=MESH,
        )

    def arrived(a, way, h, which):
        hop(a, way, h, which).wait_recv()
        return at_pos(pos - ways[way][0] * h)

    def begin(a):
        for which in (0, 1):
            for way in (0, 1):
                hop(a, way, 1, which).start()

    begin(0)

    def count_copy(j):
        return pltpu.make_async_remote_copy(
            src_ref=counts.at[dp],
            dst_ref=counts.at[dp],
            send_sem=ct_send.at[j],
            recv_sem=ct_recv.at[j],
            device_id={"dp": lax.rem(dp + j, ndp)},
            device_id_type=MESH,
        )

    for j in range(1, ndp):
        count_copy(j).start()

    W, U = 256, 4
    logs = (s_log, t_log)
    alls = (s_all, t_all)

    def rows_of(block):
        return pl.ds(pl.multiple_of(block * F, F), F)

    def accumulate(a, log, blocks, everything):
        half = slice(a * C, (a + 1) * C)

        def tile(i):
            for u in range(U):
                span = pl.ds(pl.multiple_of((i * U + u) * W, W), W)
                total = log[half, span]
                for block in blocks:
                    total = total + jnp.dot(
                        everything[a, block], head[rows_of(block), span], preferred_element_type=F32
                    )
                log[half, span] = total

        loop(0, V // (W * U), tile)

    def first(log, own):
        def tile(i):
            for u in range(U):
                span = pl.ds(pl.multiple_of((i * U + u) * W, W), W)
                log[:, span] = jnp.dot(own[...], head[rows_of(me), span], preferred_element_type=F32)

        loop(0, V // (W * U), tile)

    def take(a, h, which):
        found = []
        for way in (0, 1):
            if isinstance(h, int) and h == H and way != which:
                continue
            found.append(arrived(a, way, h, which))
            if isinstance(h, int):
                if h < H and (way == which or h + 1 < H):
                    hop(a, way, h + 1, which).start()
            else:
                hop(a, way, h + 1, which).start()
        accumulate(a, logs[which], found, alls[which])

    R = 16
    lane = lax.broadcasted_iota(jnp.int32, (R, 128), 1)

    def softmax_rows(r):
        span = pl.ds(pl.multiple_of(r * R, R), R)
        s, t = s_log[span, :], t_log[span, :]
        s_peak = jnp.max(s, axis=1, keepdims=True)
        t_peak = jnp.max(t, axis=1, keepdims=True)
        s_exp = jnp.exp(s - s_peak)
        t_exp = jnp.exp(t - t_peak)
        cross = jnp.sum(t_exp * (t - s), axis=1, keepdims=True)
        s_log[span, :] = s_exp
        t_log[span, :] = t_exp
        s_sum = jnp.sum(s_exp, axis=1, keepdims=True)
        t_sum = jnp.sum(t_exp, axis=1, keepdims=True)
        value = jnp.where(lane == 0, s_peak, jnp.where(lane == 1, s_sum, jnp.where(
            lane == 2, t_peak, jnp.where(lane == 3, t_sum, cross))))
        cols[span, :] = value

    def softmax(a, part):
        loop((a * C + part * E) // R, (a * C + part * E + E) // R, softmax_rows, 2)

    def stat_copy(a, j):
        return pltpu.make_async_remote_copy(
            src_ref=stats.at[a, me],
            dst_ref=stats.at[a, me],
            send_sem=st_send.at[a, j],
            recv_sem=st_recv.at[a, j],
            device_id={"vocab": lax.rem(me + j, n)},
            device_id_type=MESH,
        )

    def tell(a):
        stats[a, me] = cols[a * C:(a + 1) * C, :].T[:8, :]
        for j in range(1, n):
            stat_copy(a, j).start()

    def slope_rows(r):
        span = pl.ds(pl.multiple_of(r * R, R), R)
        slopes[span, :] = (s_log[span, :] * cols[span, 0:1] - t_log[span, :] * cols[span, 1:2]).astype(BF16)

    def merge(a):
        half = slice(a * C, (a + 1) * C)
        if a == 0:
            for j in range(1, ndp):
                count_copy(j).wait_recv()
        total = counts[0, :1, :1]
        for j in range(1, ndp):
            total = total + counts[j, :1, :1]
        segments = steps_ref.shape[0] // 2
        factor = jnp.concatenate(
            [
                STEPS / jnp.full((1, C // segments), steps_ref[a * segments + i], jnp.int32).astype(F32)
                for i in range(segments)
            ],
            axis=1,
        )
        weight = mask_ref[:, half].astype(F32) * factor * (T * ndp / jnp.maximum(total, 1.0))
        for j in range(1, n):
            stat_copy(a, j).wait_recv()
        s_top = stats[a, 0, 0:1, :]
        t_top = stats[a, 0, 2:3, :]
        for k in range(1, n):
            s_top = jnp.maximum(s_top, stats[a, k, 0:1, :])
            t_top = jnp.maximum(t_top, stats[a, k, 2:3, :])
        s_total = jnp.zeros((1, C), F32)
        t_total = jnp.zeros((1, C), F32)
        cross = jnp.zeros((1, C), F32)
        for k in range(n):
            t_scale = jnp.exp(stats[a, k, 2:3, :] - t_top)
            s_total += stats[a, k, 1:2, :] * jnp.exp(stats[a, k, 0:1, :] - s_top)
            t_total += stats[a, k, 3:4, :] * t_scale
            cross += stats[a, k, 4:5, :] * t_scale
        div_ref[:, half] = cross / t_total - (t_top + jnp.log(t_total)) + (s_top + jnp.log(s_total))
        mine = stats[a, me]
        s_factor = weight * (jnp.exp(mine[0:1, :] - s_top) / s_total)
        t_factor = weight * (jnp.exp(mine[2:3, :] - t_top) / t_total)
        row = lax.broadcasted_iota(jnp.int32, (128, C), 0)
        cols[half, :] = jnp.where(row == 0, s_factor, t_factor).T
        loop(a * C // R, (a + 1) * C // R, slope_rows, 4)

    def part(a, block):
        return lax.dot_general(
            slopes[a * C:(a + 1) * C, :], head[rows_of(block), :], (((1,), (1,)), ((), ())),
            preferred_element_type=F32,
        )

    def pass_on(a, way, k, c):
        return pltpu.make_async_remote_copy(
            src_ref=rs_out.at[a, way, k, c],
            dst_ref=rs_in.at[a, way, k, c],
            send_sem=rs_send.at[a, way, k, c],
            recv_sem=rs_recv.at[a, way, k, c],
            device_id={"vocab": ways[way][1]},
            device_id_type=MESH,
        )

    def far(a):
        whole = part(a, at_pos(pos + H)).astype(BF16)
        for c in (0, 1):
            rs_out[a, c, H, c] = whole[c * E:(c + 1) * E]
            pass_on(a, c, H, c).start()

    def fill(a, k):
        for way in (0, 1):
            whole = part(a, at_pos(pos + ways[way][0] * k))
            g[way, k, 0] = whole[:E]
            g[way, k, 1] = whole[E:]

    def own(a):
        whole = part(a, me)
        g[0, 0, 0] = whole[:E]
        g[0, 0, 1] = whole[E:]

    def relay_top(a):
        k = H - 1
        for way in (0, 1):
            c = 1 - way
            rs_out[a, way, k, c] = g[way, k, c].astype(BF16)
            pass_on(a, way, k, c).start()
        for way in (0, 1):
            pass_on(a, way, H, way).wait_recv()
            rs_out[a, way, k, way] = (g[way, k, way] + rs_in[a, way, H, way].astype(F32)).astype(BF16)
            pass_on(a, way, k, way).start()

    def relay(a, k):
        for late in (0, 1):
            for way in (0, 1):
                c = 1 - way if late == 0 else way
                pass_on(a, way, k + 1, c).wait_recv()
                rs_out[a, way, k, c] = (g[way, k, c] + rs_in[a, way, k + 1, c].astype(F32)).astype(BF16)
                pass_on(a, way, k, c).start()

    def finish(a):
        for c in (0, 1):
            for way in (0, 1):
                pass_on(a, way, 1, c).wait_recv()
            grad_ref[a * C + c * E:a * C + (c + 1) * E, :] = (
                g[0, 0, c] + rs_in[a, 0, 1, c].astype(F32) + rs_in[a, 1, 1, c].astype(F32)
            ).astype(BF16)

    head_copy.wait()
    first(s_log, s_ref)
    first(t_log, t_ref)

    loop(1, H - 1, lambda h: [take(0, h, which) for which in (0, 1)])
    for which in (0, 1):
        take(0, H - 1, which)
    begin(1)
    for which in (0, 1):
        take(0, H, which)

    take(1, 1, 0)
    softmax(0, 0)
    take(1, 1, 1)
    softmax(0, 1)
    tell(0)
    loop(2, H - 1, lambda h: [take(1, h, which) for which in (0, 1)])
    take(1, H - 1, 0)
    merge(0)
    take(1, H - 1, 1)
    far(0)
    fill(0, H - 1)
    take(1, H, 0)
    loop(1, H - 1, lambda k: fill(0, k))
    take(1, H, 1)
    relay_top(0)

    lower = list(range(H - 2, 0, -1))
    cut = len(lower) // 2
    softmax(1, 0)
    for k in lower[:cut]:
        relay(0, k)
    softmax(1, 1)
    tell(1)
    for k in lower[cut:]:
        relay(0, k)
    own(0)
    merge(1)
    far(1)
    finish(0)
    fill(1, H - 1)
    relay_top(1)

    def rest(i):
        fill(1, H - 2 - i)
        relay(1, H - 2 - i)

    loop(0, H - 2, rest)
    own(1)
    finish(1)

    for a in (0, 1):
        def left(h):
            for way in (0, 1):
                for which in (0, 1):
                    hop(a, way, h, which).wait_send()

        def gone(k):
            for way in (0, 1):
                for c in (0, 1):
                    pass_on(a, way, k, c).wait_send()

        left(1)
        loop(2, H, left)
        loop(1, H, gone)
        for way in (0, 1):
            hop(a, way, H, way).wait_send()
            pass_on(a, way, H, way).wait_send()
        for j in range(1, n):
            stat_copy(a, j).wait_send()
    for j in range(1, ndp):
        count_copy(j).wait_send()


def solution(mesh):
    n, ndp = mesh.shape["vocab"], mesh.shape["dp"]

    def per_device(student, teacher, head, mask, steps):
        T, F = student.shape
        D, V = head.shape
        H = n // 2
        vmem = pl.BlockSpec(memory_space=pltpu.VMEM)
        dma = pltpu.SemaphoreType.DMA
        div, grad = pl.pallas_call(
            functools.partial(kernel, n, ndp),
            out_shape=(jax.ShapeDtypeStruct((1, T), F32), jax.ShapeDtypeStruct((T, F), BF16)),
            in_specs=[vmem, vmem, pl.BlockSpec(memory_space=pl.ANY), vmem, pl.BlockSpec(memory_space=pltpu.SMEM)],
            out_specs=(vmem, vmem),
            scratch_shapes=[
                pltpu.VMEM((D, V), BF16),
                pltpu.VMEM((2, n, T // 2, F), BF16),
                pltpu.VMEM((2, n, T // 2, F), BF16),
                pltpu.VMEM((T, V), F32),
                pltpu.VMEM((T, V), F32),
                pltpu.VMEM((T, V), BF16),
                pltpu.VMEM((T, 128), F32),
                pltpu.VMEM((2, n, 8, T // 2), F32),
                pltpu.VMEM((ndp, 8, 128), F32),
                pltpu.VMEM((2, H, 2, T // 4, F), F32),
                pltpu.VMEM((2, 2, H + 1, 2, T // 4, F), BF16),
                pltpu.VMEM((2, 2, H + 1, 2, T // 4, F), BF16),
                dma,
                dma((2, 2, H + 1, 2)),
                dma((2, 2, H + 1, 2)),
                dma((2, n)),
                dma((2, n)),
                dma((ndp,)),
                dma((ndp,)),
                dma((2, 2, H + 1, 2)),
                dma((2, 2, H + 1, 2)),
            ],
            compiler_params=pltpu.CompilerParams(
                collective_id=0, has_side_effects=True, vmem_limit_bytes=60 * 1024 * 1024
            ),
        )(student, teacher, head, mask.reshape(1, T), steps)
        return div.reshape(T), grad

    return jax.shard_map(
        per_device,
        mesh=mesh,
        in_specs=(P("dp", "vocab"), P("dp", "vocab"), P(None, "vocab"), P("dp"), P("dp")),
        out_specs=(P("dp"), P("dp", "vocab")),
        check_vma=False,
    )
```

```python
import functools

import jax
import jax.numpy as jnp
from jax import lax
from jax.experimental import pallas as pl
from jax.experimental.pallas import tpu as pltpu
from jax.sharding import PartitionSpec as P

MESH = pl.DeviceIdType.MESH
STEPS = 8
F32, BF16 = jnp.float32, jnp.bfloat16


def loop(start, stop, body, unroll=1):
    lax.fori_loop(start, stop, lambda i, carry: (body(i), carry)[1], 0, unroll=unroll)


def kernel(
    n, ndp, s_ref, t_ref, head_hbm, mask_ref, steps_ref, div_ref, grad_ref,
    head, s_all, t_all, s_log, t_log, slopes, cols, stats, counts, g, rs_out, rs_in,
    head_sem, ag_send, ag_recv, st_send, st_recv, ct_send, ct_recv, rs_send, rs_recv,
):
    T, F = s_ref.shape
    V = head.shape[1]
    H = n // 2
    C = T // 2
    E = C // 2
    me = lax.axis_index("vocab")
    dp = lax.axis_index("dp")

    def at_pos(q):
        q = lax.rem(q + 2 * n, n)
        x = q // H
        z = q + x * (n - 1 - 2 * q)
        return 2 * z + x

    z0, x0 = me // 2, lax.rem(me, 2)
    pos = z0 + x0 * (n - 1 - 2 * z0)
    ways = ((1, at_pos(pos + 1)), (-1, at_pos(pos - 1)))

    head_copy = pltpu.make_async_copy(head_hbm, head, head_sem)
    head_copy.start()

    count = jnp.sum(mask_ref[...].astype(F32), axis=1, keepdims=True)
    counts[dp] = jnp.broadcast_to(count, counts.shape[1:])

    barrier = pltpu.get_barrier_semaphore()
    for j in range(1, n):
        pl.semaphore_signal(barrier, 1, device_id={"vocab": lax.rem(me + j, n)}, device_id_type=MESH)
    for j in range(1, ndp):
        pl.semaphore_signal(barrier, 1, device_id={"dp": lax.rem(dp + j, ndp)}, device_id_type=MESH)
    pl.semaphore_wait(barrier, n - 1 + ndp - 1)

    def hop(a, way, h, which):
        step, target = ways[way]
        block = at_pos(pos - step * (h - 1))
        everything, own = ((s_all, s_ref), (t_all, t_ref))[which]
        source = own.at[a * C:(a + 1) * C] if isinstance(h, int) and h == 1 else everything.at[a, block]
        return pltpu.make_async_remote_copy(
            src_ref=source,
            dst_ref=everything.at[a, block],
            send_sem=ag_send.at[a, way, h, which],
            recv_sem=ag_recv.at[a, way, h, which],
            device_id={"vocab": target},
            device_id_type=MESH,
        )

    def arrived(a, way, h, which):
        hop(a, way, h, which).wait_recv()
        return at_pos(pos - ways[way][0] * h)

    def begin(a):
        for which in (0, 1):
            for way in (0, 1):
                hop(a, way, 1, which).start()

    begin(0)

    def count_copy(j):
        return pltpu.make_async_remote_copy(
            src_ref=counts.at[dp],
            dst_ref=counts.at[dp],
            send_sem=ct_send.at[j],
            recv_sem=ct_recv.at[j],
            device_id={"dp": lax.rem(dp + j, ndp)},
            device_id_type=MESH,
        )

    for j in range(1, ndp):
        count_copy(j).start()

    W, U = 256, 4
    logs = (s_log, t_log)
    alls = (s_all, t_all)

    def rows_of(block):
        return pl.ds(pl.multiple_of(block * F, F), F)

    def accumulate(a, log, blocks, everything):
        half = slice(a * C, (a + 1) * C)

        def tile(i):
            for u in range(U):
                span = pl.ds(pl.multiple_of((i * U + u) * W, W), W)
                total = log[half, span]
                for block in blocks:
                    total = total + jnp.dot(
                        everything[a, block], head[rows_of(block), span], preferred_element_type=F32
                    )
                log[half, span] = total

        loop(0, V // (W * U), tile)

    def first(log, own):
        def tile(i):
            for u in range(U):
                span = pl.ds(pl.multiple_of((i * U + u) * W, W), W)
                log[:, span] = jnp.dot(own[...], head[rows_of(me), span], preferred_element_type=F32)

        loop(0, V // (W * U), tile)

    def take(a, h, which):
        found = []
        for way in (0, 1):
            if isinstance(h, int) and h == H and way != which:
                continue
            found.append(arrived(a, way, h, which))
            if isinstance(h, int):
                if h < H and (way == which or h + 1 < H):
                    hop(a, way, h + 1, which).start()
            else:
                hop(a, way, h + 1, which).start()
        accumulate(a, logs[which], found, alls[which])

    R = 16
    lane = lax.broadcasted_iota(jnp.int32, (R, 128), 1)

    def softmax_rows(r):
        span = pl.ds(pl.multiple_of(r * R, R), R)
        s, t = s_log[span, :], t_log[span, :]
        s_peak = jnp.max(s, axis=1, keepdims=True)
        t_peak = jnp.max(t, axis=1, keepdims=True)
        s_exp = jnp.exp(s - s_peak)
        t_exp = jnp.exp(t - t_peak)
        cross = jnp.sum(t_exp * (t - s), axis=1, keepdims=True)
        s_log[span, :] = s_exp
        t_log[span, :] = t_exp
        s_sum = jnp.sum(s_exp, axis=1, keepdims=True)
        t_sum = jnp.sum(t_exp, axis=1, keepdims=True)
        value = jnp.where(lane == 0, s_peak, jnp.where(lane == 1, s_sum, jnp.where(
            lane == 2, t_peak, jnp.where(lane == 3, t_sum, cross))))
        cols[span, :] = value

    def softmax(a, part):
        loop((a * C + part * E) // R, (a * C + part * E + E) // R, softmax_rows, 2)

    def stat_copy(a, j):
        return pltpu.make_async_remote_copy(
            src_ref=stats.at[a, me],
            dst_ref=stats.at[a, me],
            send_sem=st_send.at[a, j],
            recv_sem=st_recv.at[a, j],
            device_id={"vocab": lax.rem(me + j, n)},
            device_id_type=MESH,
        )

    def tell(a):
        stats[a, me] = cols[a * C:(a + 1) * C, :].T[:8, :]
        for j in range(1, n):
            stat_copy(a, j).start()

    def slope_rows(r):
        span = pl.ds(pl.multiple_of(r * R, R), R)
        slopes[span, :] = (s_log[span, :] * cols[span, 0:1] - t_log[span, :] * cols[span, 1:2]).astype(BF16)

    def merge(a):
        half = slice(a * C, (a + 1) * C)
        if a == 0:
            for j in range(1, ndp):
                count_copy(j).wait_recv()
        total = counts[0, :1, :1]
        for j in range(1, ndp):
            total = total + counts[j, :1, :1]
        segments = steps_ref.shape[0] // 2
        factor = jnp.concatenate(
            [
                STEPS / jnp.full((1, C // segments), steps_ref[a * segments + i], jnp.int32).astype(F32)
                for i in range(segments)
            ],
            axis=1,
        )
        weight = mask_ref[:, half].astype(F32) * factor * (T * ndp / jnp.maximum(total, 1.0))
        for j in range(1, n):
            stat_copy(a, j).wait_recv()
        s_top = stats[a, 0, 0:1, :]
        t_top = stats[a, 0, 2:3, :]
        for k in range(1, n):
            s_top = jnp.maximum(s_top, stats[a, k, 0:1, :])
            t_top = jnp.maximum(t_top, stats[a, k, 2:3, :])
        s_total = jnp.zeros((1, C), F32)
        t_total = jnp.zeros((1, C), F32)
        cross = jnp.zeros((1, C), F32)
        for k in range(n):
            t_scale = jnp.exp(stats[a, k, 2:3, :] - t_top)
            s_total += stats[a, k, 1:2, :] * jnp.exp(stats[a, k, 0:1, :] - s_top)
            t_total += stats[a, k, 3:4, :] * t_scale
            cross += stats[a, k, 4:5, :] * t_scale
        div_ref[:, half] = cross / t_total - (t_top + jnp.log(t_total)) + (s_top + jnp.log(s_total))
        mine = stats[a, me]
        s_factor = weight * (jnp.exp(mine[0:1, :] - s_top) / s_total)
        t_factor = weight * (jnp.exp(mine[2:3, :] - t_top) / t_total)
        row = lax.broadcasted_iota(jnp.int32, (128, C), 0)
        cols[half, :] = jnp.where(row == 0, s_factor, t_factor).T
        loop(a * C // R, (a + 1) * C // R, slope_rows, 4)

    def part(a, block):
        return lax.dot_general(
            slopes[a * C:(a + 1) * C, :], head[rows_of(block), :], (((1,), (1,)), ((), ())),
            preferred_element_type=F32,
        )

    def pass_on(a, way, k, c):
        return pltpu.make_async_remote_copy(
            src_ref=rs_out.at[a, way, k, c],
            dst_ref=rs_in.at[a, way, k, c],
            send_sem=rs_send.at[a, way, k, c],
            recv_sem=rs_recv.at[a, way, k, c],
            device_id={"vocab": ways[way][1]},
            device_id_type=MESH,
        )

    def far(a):
        whole = part(a, at_pos(pos + H)).astype(BF16)
        for c in (0, 1):
            rs_out[a, c, H, c] = whole[c * E:(c + 1) * E]
            pass_on(a, c, H, c).start()

    def fill(a, k):
        for way in (0, 1):
            whole = part(a, at_pos(pos + ways[way][0] * k))
            g[way, k, 0] = whole[:E]
            g[way, k, 1] = whole[E:]

    def own(a):
        whole = part(a, me)
        g[0, 0, 0] = whole[:E]
        g[0, 0, 1] = whole[E:]

    def relay_top(a):
        k = H - 1
        for way in (0, 1):
            c = 1 - way
            rs_out[a, way, k, c] = g[way, k, c].astype(BF16)
            pass_on(a, way, k, c).start()
        for way in (0, 1):
            pass_on(a, way, H, way).wait_recv()
            rs_out[a, way, k, way] = (g[way, k, way] + rs_in[a, way, H, way].astype(F32)).astype(BF16)
            pass_on(a, way, k, way).start()

    def relay(a, k):
        for late in (0, 1):
            for way in (0, 1):
                c = 1 - way if late == 0 else way
                pass_on(a, way, k + 1, c).wait_recv()
                rs_out[a, way, k, c] = (g[way, k, c] + rs_in[a, way, k + 1, c].astype(F32)).astype(BF16)
                pass_on(a, way, k, c).start()

    def finish(a):
        for c in (0, 1):
            for way in (0, 1):
                pass_on(a, way, 1, c).wait_recv()
            grad_ref[a * C + c * E:a * C + (c + 1) * E, :] = (
                g[0, 0, c] + rs_in[a, 0, 1, c].astype(F32) + rs_in[a, 1, 1, c].astype(F32)
            ).astype(BF16)

    head_copy.wait()
    first(s_log, s_ref)
    first(t_log, t_ref)

    loop(1, H - 1, lambda h: [take(0, h, which) for which in (0, 1)])
    for which in (0, 1):
        take(0, H - 1, which)
    begin(1)
    for which in (0, 1):
        take(0, H, which)

    take(1, 1, 0)
    softmax(0, 0)
    take(1, 1, 1)
    softmax(0, 1)
    tell(0)
    loop(2, H - 1, lambda h: [take(1, h, which) for which in (0, 1)])
    take(1, H - 1, 0)
    merge(0)
    take(1, H - 1, 1)
    far(0)
    fill(0, H - 1)
    take(1, H, 0)
    loop(1, H - 1, lambda k: fill(0, k))
    take(1, H, 1)
    relay_top(0)

    lower = list(range(H - 2, 0, -1))
    softmax(1, 0)
    softmax(1, 1)
    tell(1)
    for k in lower[:-1]:
        relay(0, k)
    own(0)
    merge(1)
    far(1)
    for k in lower[-1:]:
        relay(0, k)
    fill(1, H - 1)
    relay_top(1)

    def rest(i):
        fill(1, H - 2 - i)
        relay(1, H - 2 - i)

    loop(0, H - 2, rest)
    finish(0)
    own(1)
    finish(1)

    for a in (0, 1):
        def left(h):
            for way in (0, 1):
                for which in (0, 1):
                    hop(a, way, h, which).wait_send()

        def gone(k):
            for way in (0, 1):
                for c in (0, 1):
                    pass_on(a, way, k, c).wait_send()

        left(1)
        loop(2, H, left)
        loop(1, H, gone)
        for way in (0, 1):
            hop(a, way, H, way).wait_send()
            pass_on(a, way, H, way).wait_send()
        for j in range(1, n):
            stat_copy(a, j).wait_send()
    for j in range(1, ndp):
        count_copy(j).wait_send()


def solution(mesh):
    n, ndp = mesh.shape["vocab"], mesh.shape["dp"]

    def per_device(student, teacher, head, mask, steps):
        T, F = student.shape
        D, V = head.shape
        H = n // 2
        vmem = pl.BlockSpec(memory_space=pltpu.VMEM)
        dma = pltpu.SemaphoreType.DMA
        div, grad = pl.pallas_call(
            functools.partial(kernel, n, ndp),
            out_shape=(jax.ShapeDtypeStruct((1, T), F32), jax.ShapeDtypeStruct((T, F), BF16)),
            in_specs=[vmem, vmem, pl.BlockSpec(memory_space=pl.ANY), vmem, pl.BlockSpec(memory_space=pltpu.SMEM)],
            out_specs=(vmem, vmem),
            scratch_shapes=[
                pltpu.VMEM((D, V), BF16),
                pltpu.VMEM((2, n, T // 2, F), BF16),
                pltpu.VMEM((2, n, T // 2, F), BF16),
                pltpu.VMEM((T, V), F32),
                pltpu.VMEM((T, V), F32),
                pltpu.VMEM((T, V), BF16),
                pltpu.VMEM((T, 128), F32),
                pltpu.VMEM((2, n, 8, T // 2), F32),
                pltpu.VMEM((ndp, 8, 128), F32),
                pltpu.VMEM((2, H, 2, T // 4, F), F32),
                pltpu.VMEM((2, 2, H + 1, 2, T // 4, F), BF16),
                pltpu.VMEM((2, 2, H + 1, 2, T // 4, F), BF16),
                dma,
                dma((2, 2, H + 1, 2)),
                dma((2, 2, H + 1, 2)),
                dma((2, n)),
                dma((2, n)),
                dma((ndp,)),
                dma((ndp,)),
                dma((2, 2, H + 1, 2)),
                dma((2, 2, H + 1, 2)),
            ],
            compiler_params=pltpu.CompilerParams(
                collective_id=0, has_side_effects=True, vmem_limit_bytes=60 * 1024 * 1024
            ),
        )(student, teacher, head, mask.reshape(1, T), steps)
        return div.reshape(T), grad

    return jax.shard_map(
        per_device,
        mesh=mesh,
        in_specs=(P("dp", "vocab"), P("dp", "vocab"), P(None, "vocab"), P("dp"), P("dp")),
        out_specs=(P("dp"), P("dp", "vocab")),
        check_vma=False,
    )
```
